256 devices in a mesh: ctx: 64 (over x, z, y_hi), tp: 4 (over y_lo, core).
Axes of the slice: x: 4, y: 4 (y_hi: 2, y_lo: 2; y = y_hi * 2 + y_lo), z: 8, core: 2. Of those that a mesh axis runs over, the one named last changes fastest.
Arguments:
- q_one: bfloat16 [16384, 4096], P('ctx', 'tp'), may hold values from -880 to 880
- k_one: bfloat16 [16384, 4096], P('ctx', 'tp'), may hold values from -6 to 6
- v_one: bfloat16 [16384, 4096], P('ctx', 'tp'), may hold values from -6 to 6
- q_two: bfloat16 [16384, 4096], P('ctx', 'tp'), may hold values from -6 to 6
- k_two: bfloat16 [16384, 4096], P('ctx', 'tp'), may hold values from -6 to 6
- short_taps: bfloat16 [3, 7, 256], P(None, None, 'tp'), may hold values from -2 to 2
- medium_taps: bfloat16 [128, 256], P(None, 'tp'), may hold values from -0.5 to 0.5
- long_taps: bfloat16 [256, 16384], P('tp', 'ctx'), may hold values from -0.046875 to 0.046875
- skip_gain: float32 [4096], P('tp'), may hold values from -4 to 4
- block_order: int32 [64], replicated, may hold values from 0 to 63, as said below
- prev_owner: int32 [64], replicated, may hold values from 0 to 63, as said below
Outputs:
- gated_out: bfloat16 [16384, 4096], P('ctx', 'tp')
The draws below stay inside these ranges and needn't reach their ends.
Inputs may be any that keep to these rules, and one draw needn't show every extreme that they name: `block_order`: A permutation of the 64 sequence blocks over the devices of ctx. prev_owner[b] is the device d with block_order[d] = b - 1 for b > 0, and prev_owner[0] the device holding block 63.
All inputs are finite; a program needn't handle non-finite values.
Results may differ from the reference program's by a relative error of at most 0.008.
Values may be sent and summed in bfloat16 or wider, within the bound.
A program may use at most 128 MiB of HBM per device.

```python
import math
import jax
import jax.numpy as jnp
from jax import lax

CH = 4096
GROUP = 16
SE = 7
MR = 128
T_DEV = 256
GROUPS = 256
SEQ = 16384
N_CTX = 64


def draw_q_one(key, part):
    noise_key, row_key, col_key = jax.random.split(key, 3)
    channel = jnp.arange(CH, dtype=jnp.float32) / CH
    noise = jax.random.truncated_normal(noise_key, -4.0, 4.0, (SEQ, CH), jnp.float32)
    ramp = 1.0 + 1.2 * channel
    row_scale = jnp.exp(jax.random.uniform(row_key, (SEQ, 1), jnp.float32, 0.0, math.log(10.0)))
    col_scale = jnp.exp(jax.random.uniform(col_key, (1, CH), jnp.float32, 0.0, math.log(10.0)))
    return (noise * row_scale * col_scale * ramp[None, :]).astype(jnp.bfloat16)


def block_layout(key):
    return jax.random.permutation(jax.random.fold_in(key, 11), N_CTX).astype(jnp.int32)


def draw_block_order(key, part):
    return block_layout(key)


def draw_prev_owner(key, part):
    order = block_layout(key)
    holder = jnp.zeros((N_CTX,), jnp.int32).at[order].set(jnp.arange(N_CTX, dtype=jnp.int32))
    return jnp.roll(holder, 1)


def block_levels(own_key, dims, pieces, smallest, high):
    level, own = 1.0, jax.random.fold_in(own_key, 6)
    for axis_at, shards_of in pieces:
        steps = jnp.exp(jax.random.uniform(jax.random.fold_in(own, axis_at), (shards_of,), jnp.float32, smallest / len(pieces), high / len(pieces)))
        level = level * jnp.repeat(steps, dims[axis_at] // shards_of).reshape([-1 if axis == axis_at else 1 for axis in range(len(dims))])
    return level


def bell_draw(rng, extent, spread, most, pieces=(), kind=jnp.bfloat16):
    result = jax.random.normal(rng, extent, jnp.float32) * spread
    if len(pieces) > 0:
        result = block_levels(rng, extent, pieces, -0.22, 0.18) * result
    return jnp.clip(result, min=-most, max=most).astype(kind)


def setup_inputs(seed: int = 0) -> dict:
    splits = jax.random.split(jax.random.key(seed), 12)
    q_one = draw_q_one(jax.random.fold_in(splits[11], 71), 0)
    k_one = bell_draw(splits[1], (SEQ, CH), 1.0, 6.0, ((0, 64), (1, 4)))
    v_one = bell_draw(splits[2], (SEQ, CH), 1.0, 6.0, ((0, 64), (1, 4)))
    q_two = bell_draw(splits[3], (SEQ, CH), 1.0, 6.0, ((0, 64), (1, 4)))
    k_two = bell_draw(splits[4], (SEQ, CH), 1.0, 6.0, ((0, 64), (1, 4)))
    short_taps = bell_draw(splits[5], (3, SE, GROUPS), SE ** -0.5, 2.0, ((2, 4),))
    medium_taps = bell_draw(splits[6], (MR, GROUPS), MR ** -0.5, 0.5, ((1, 4),))
    long_taps = bell_draw(splits[7], (GROUPS, SEQ), SEQ ** -0.5, 0.046875, ((0, 4), (1, 64)))
    skip_gain = bell_draw(splits[8], (CH,), 1.0, 4.0, ((0, 4),), jnp.float32)
    block_order = draw_block_order(jax.random.fold_in(splits[11], 71), 0)
    prev_owner = draw_prev_owner(jax.random.fold_in(splits[11], 71), 0)
    return {"q_one": q_one, "k_one": k_one, "v_one": v_one, "q_two": q_two, "k_two": k_two, "short_taps": short_taps, "medium_taps": medium_taps, "long_taps": long_taps, "skip_gain": skip_gain, "block_order": block_order, "prev_owner": prev_owner}


EPSILON = 1e-06
BLOCK_LANES = 256

def causal_filter(padded, kernel_taps):
    reach = kernel_taps.shape[0] - 1

    def add_tap(j, total):
        piece = lax.dynamic_slice_in_dim(padded, reach - j, T_DEV, axis=1).astype(jnp.float32)
        return total + piece * kernel_taps[j].astype(jnp.float32)[None, None, :]
    start_total = jnp.zeros((padded.shape[0], T_DEV, padded.shape[2]), jnp.float32)
    return lax.fori_loop(0, reach + 1, add_tap, start_total)

def with_before(blocks, source, first_block, count):
    before = blocks[source][:, T_DEV - count:]
    before = jnp.where(first_block[:, None, None], jnp.zeros_like(before), before)
    return jnp.concatenate([before, blocks], axis=1)

def long_group(group_item):
    group_taps, group_rows = group_item
    padded_len = 2 * SEQ
    spectrum = jnp.fft.rfft(group_rows, n=padded_len, axis=1) * jnp.fft.rfft(group_taps, n=padded_len)[None, :]
    return jnp.fft.irfft(spectrum, n=padded_len, axis=1)[:, :SEQ]

def reference(q_one, k_one, v_one, q_two, k_two, short_taps, medium_taps, long_taps, skip_gain, block_order, prev_owner):
    block_shape = (N_CTX, T_DEV, CH)
    col_count = CH // BLOCK_LANES
    group_count = BLOCK_LANES // GROUP
    source = prev_owner[block_order]
    first_block = block_order == 0
    short_lanes = jnp.repeat(short_taps, GROUP, axis=2)
    medium_lanes = jnp.repeat(medium_taps, GROUP, axis=1)
    q_blocks = q_one.reshape(block_shape)
    k_blocks = k_one.reshape(block_shape)
    v_blocks = v_one.reshape(block_shape)
    gate_blocks = k_two.reshape(block_shape)
    out_gate = q_two.reshape(block_shape)

    def lanes_of(array, start):
        return lax.dynamic_slice_in_dim(array, start, BLOCK_LANES, axis=2)

    def mixed_block(col):
        start = col * BLOCK_LANES
        short_here = lax.dynamic_slice_in_dim(short_lanes, start, BLOCK_LANES, axis=2)
        medium_here = lax.dynamic_slice_in_dim(medium_lanes, start, BLOCK_LANES, axis=1)
        q_feat = causal_filter(with_before(lanes_of(q_blocks, start), source, first_block, SE - 1), short_here[0])
        k_feat = causal_filter(with_before(lanes_of(k_blocks, start), source, first_block, SE - 1), short_here[1])
        v_feat = causal_filter(with_before(lanes_of(v_blocks, start), source, first_block, SE - 1), short_here[2])
        z_one = (k_feat * v_feat).astype(jnp.bfloat16)
        medium = causal_filter(with_before(z_one, source, first_block, MR - 1), medium_here)
        return q_feat * medium
    mixed_all = lax.map(mixed_block, jnp.arange(col_count, dtype=jnp.int32))
    energy = lax.optimization_barrier(jnp.sum(lax.optimization_barrier(jnp.sum(mixed_all * mixed_all, axis=3)), axis=0))
    scale = lax.rsqrt(energy / CH + EPSILON)[:, :, None]
    holder = jnp.argsort(block_order).astype(jnp.int32)

    def output_block(item):
        col, mixed = item
        start = col * BLOCK_LANES
        v_two = (lanes_of(gate_blocks, start).astype(jnp.float32) * mixed * scale).astype(jnp.bfloat16)
        ordered = v_two[holder].reshape(SEQ, BLOCK_LANES)
        lanes = jnp.transpose(ordered).astype(jnp.float32).reshape(group_count, GROUP, SEQ)
        taps_here = lax.dynamic_slice_in_dim(long_taps, col * group_count, group_count, axis=0).astype(jnp.float32)
        long_part = lax.map(long_group, (taps_here, lanes))
        long_part = jnp.transpose(long_part.reshape(BLOCK_LANES, SEQ))
        gain_here = lax.dynamic_slice_in_dim(skip_gain, start, BLOCK_LANES)
        mixed_seq = (long_part + gain_here[None, :] * ordered.astype(jnp.float32)).astype(jnp.bfloat16)
        placed = mixed_seq.reshape(N_CTX, T_DEV, BLOCK_LANES)[block_order]
        return (lanes_of(out_gate, start).astype(jnp.float32) * placed.astype(jnp.float32)).astype(jnp.bfloat16)
    outputs = lax.map(output_block, (jnp.arange(col_count, dtype=jnp.int32), mixed_all))
    return jnp.transpose(outputs, (1, 2, 0, 3)).reshape(SEQ, CH)
```

```python
import functools

import jax
import jax.numpy as jnp
from jax import lax
from jax.experimental import pallas as pl
from jax.experimental.pallas import tpu as pltpu
from jax.sharding import PartitionSpec as P

EPSILON = 1e-06
LANES = 128
GROUP = 16
F32 = jnp.float32
BF16 = jnp.bfloat16
VMEM_LIMIT = 60 * 1024 * 1024


def iota(shape, dim):
    return lax.broadcasted_iota(jnp.int32, shape, dim)


def spread_taps(taps, tile):
    groups = taps.shape[1]
    pick = iota((groups, LANES), 0) == tile * (LANES // GROUP) + iota((groups, LANES), 1) // GROUP
    return jnp.dot(taps.astype(F32), pick.astype(F32), preferred_element_type=F32)


def skewed(row):
    return pltpu.roll(jnp.broadcast_to(row, (LANES, LANES)), 0, 1, stride=1, stride_axis=0)


def tail_kernel(q_ref, k_ref, v_ref, short_ref, out_ref):
    rows = k_ref.shape[0]
    lead = short_ref.shape[1] - 1
    start = rows - LANES - 8

    def tile_step(tile, _):
        lanes = pl.ds(pl.multiple_of(tile * LANES, LANES), LANES)
        features = []
        for which, ref in ((1, k_ref), (2, v_ref)):
            taps = spread_taps(short_ref[which], tile)
            signal = ref[pl.ds(start, LANES + 8), lanes].astype(F32)
            total = jnp.zeros((LANES, LANES), F32)
            for j in range(lead + 1):
                total += signal[8 - j : 8 - j + LANES] * taps[j : j + 1]
            features.append(total)
        z_tail = (features[0] * features[1]).astype(BF16)
        ends = [ref[pl.ds(rows - 8, 8), lanes].astype(F32)[8 - lead :] for ref in (q_ref, k_ref, v_ref)]
        ends = jnp.concatenate(ends + [jnp.zeros((6, LANES), F32)], axis=0)
        for a in range(8):
            out_ref[a * 8 + tile, 0:16, :] = z_tail[16 * a : 16 * a + 16]
            piece = jnp.concatenate([ends[3 * a : 3 * a + 3], jnp.zeros((5, LANES), F32)], axis=0)
            out_ref[a * 8 + tile, 16:24, :] = piece.astype(BF16)
        return 0

    lax.fori_loop(0, k_ref.shape[1] // LANES, tile_step, 0)


def mix_kernel(flag_ref, q_ref, k_ref, v_ref, k_two_ref, short_ref, medium_ref, tail_ref, out_ref, energy_ref, toeplitz, signal, z_pad):
    rows, width = q_ref.shape
    lead = short_ref.shape[1] - 1
    before = (flag_ref[0] > 0).astype(F32)
    reach = medium_ref.shape[0]
    flip = (iota((reach, reach), 0) == (reach - iota((reach, reach), 1)) % reach).astype(F32)
    turned = lax.dot_general(medium_ref[...].astype(F32), flip, (((0,), (0,)), ((), ())), preferred_element_type=F32)
    z_pad_groups = turned.shape[0]
    row_at, col_at = iota((LANES, LANES), 0), iota((LANES, LANES), 1)

    def tile_step(tile, energy):
        lanes = pl.ds(pl.multiple_of(tile * LANES, LANES), LANES)
        ends = jnp.concatenate([tail_ref[a * 8 + tile].astype(F32)[16:19] for a in range(6)], axis=0) * before
        features = []
        for which, ref in enumerate((q_ref, k_ref, v_ref)):
            taps = spread_taps(short_ref[which], tile)
            signal[0:8, :] = jnp.concatenate([jnp.zeros((8 - lead, LANES), F32), ends[which * lead : (which + 1) * lead]], axis=0)
            signal[8 : 8 + rows, :] = ref[:, lanes].astype(F32)
            total = jnp.zeros((rows, LANES), F32)
            for j in range(lead + 1):
                total += signal[8 - j : 8 - j + rows, :] * taps[j : j + 1]
            features.append(total)
        for a in range(8):
            z_pad[16 * a : 16 * a + 16, :] = (tail_ref[a * 8 + tile].astype(F32)[0:16] * before).astype(BF16)
        z_pad[LANES : LANES + rows, :] = (features[1] * features[2]).astype(BF16)
        picked = (iota((z_pad_groups, LANES), 0) // 8 == tile)
        for g in range(8):
            row = jnp.sum(jnp.where(iota((z_pad_groups, LANES), 0) == tile * 8 + g, turned, 0.0), axis=0, keepdims=True)
            skew = skewed(row)
            toeplitz[g * LANES : (g + 1) * LANES, 0:LANES] = jnp.where(col_at > row_at, skew, 0.0).astype(BF16)
            toeplitz[g * LANES : (g + 1) * LANES, LANES : 2 * LANES] = jnp.where(col_at <= row_at, skew, 0.0).astype(BF16)
        stacked = jnp.concatenate([z_pad[0:rows, :], z_pad[LANES : LANES + rows, :]], axis=1)
        product = jnp.dot(toeplitz[...], stacked, preferred_element_type=F32)
        owner = iota((LANES, 2 * LANES), 1) % LANES // GROUP
        medium = jnp.zeros((LANES, 2 * LANES), F32)
        for g in range(8):
            medium = jnp.where(owner == g, product[g * LANES : (g + 1) * LANES], medium)
        medium = jnp.concatenate([medium[:, :LANES], medium[:, LANES:]], axis=0)
        mixed = features[0] * medium
        out_ref[lanes, :] = jnp.transpose(mixed * k_two_ref[:, lanes].astype(F32))
        return energy + mixed * mixed

    energy = lax.fori_loop(0, width // LANES, tile_step, jnp.zeros((rows, LANES), F32))
    energy_ref[...] = jnp.sum(jnp.transpose(energy), axis=0, keepdims=True)


def long_kernel(holder_ref, order_ref, x_ref, taps_ref, gain_ref, out_ref, x_pad, toeplitz, total):
    blocks, channels, span = x_ref.shape
    size = blocks * channels
    quarter = size // 4
    x_pad[0:quarter, :] = jnp.zeros((quarter, span), BF16)

    def place(i, _):
        x_pad[pl.ds(pl.multiple_of(quarter + i * channels, channels), channels), :] = x_ref[holder_ref[i]]
        return 0

    lax.fori_loop(0, blocks, place, 0)
    row_at, col_at = iota((LANES, LANES), 0), iota((LANES, LANES), 1)
    toeplitz[:, 0:LANES] = jnp.zeros((LANES, LANES), BF16)

    def spread(k, last):
        row = taps_ref[k].astype(F32)
        first, second = skewed(row[:, :LANES]), skewed(row[:, LANES:])
        at = pl.multiple_of(LANES + k * span, LANES)
        toeplitz[:, pl.ds(at, LANES)] = jnp.where(col_at >= row_at, first, last).astype(BF16)
        toeplitz[:, pl.ds(at + LANES, LANES)] = jnp.where(col_at >= row_at, second, first).astype(BF16)
        return second

    lax.fori_loop(0, blocks, spread, jnp.zeros((LANES, LANES), F32))
    gain = gain_ref[...]
    step = 4
    for r in range(4):
        base = quarter * (r + 1)
        own = x_pad[base : base + quarter, :].astype(F32).reshape(quarter // channels, channels, span)
        total[...] = (own * gain[None]).reshape(quarter, span)

        def add(n, _):
            left, right = [], []
            for s in range(step):
                k = n * step + s
                left.append(x_pad[pl.ds(pl.multiple_of(base - k * channels, channels), quarter), :])
                at = pl.multiple_of(LANES + k * span, LANES)
                right.append(toeplitz[:, pl.ds(at, span)])
                right.append(toeplitz[:, pl.ds(pl.multiple_of(at - LANES, LANES), span)])
            total[...] += jnp.dot(jnp.concatenate(left, axis=1), jnp.concatenate(right, axis=0), preferred_element_type=F32)
            return 0

        lax.fori_loop(0, (r + 1) * (quarter // channels) // step, add, 0)
        out_ref[r * (quarter // channels) : (r + 1) * (quarter // channels)] = total[...].astype(BF16).reshape(quarter // channels, channels, span)


def gate_kernel(y_ref, q_two_ref, out_ref):
    blocks, channels, span = y_ref.shape
    per_tile = LANES // channels

    def tile_step(tile, _):
        lanes = pl.ds(pl.multiple_of(tile * LANES, LANES), LANES)
        piece = y_ref[pl.ds(tile * per_tile, per_tile)].astype(F32).reshape(LANES, span)
        out_ref[:, lanes] = (jnp.transpose(piece) * q_two_ref[:, lanes].astype(F32)).astype(BF16)
        return 0

    lax.fori_loop(0, q_two_ref.shape[1] // LANES, tile_step, 0)


VM = pl.BlockSpec(memory_space=pltpu.VMEM)
SM = pl.BlockSpec(memory_space=pltpu.SMEM)
PARAMS = pltpu.CompilerParams(vmem_limit_bytes=VMEM_LIMIT)


def per_device(q_one, k_one, v_one, q_two, k_two, short_taps, medium_taps, long_taps, skip_gain, block_order, prev_owner):
    rows, width = q_one.shape
    ctx_count = lax.axis_size("ctx")
    me = lax.axis_index("ctx")
    lane_width = width // ctx_count
    full_width = width * lax.axis_size("tp")
    slots = jnp.arange(ctx_count, dtype=jnp.int32)
    holder = jnp.sum(jnp.where(block_order[None, :] == slots[:, None], slots[None, :], 0), axis=1)
    source = prev_owner[block_order]

    long_rows = lax.all_to_all(long_taps, "ctx", split_axis=0, concat_axis=0, tiled=True).reshape(ctx_count, 1, rows)
    tails = pl.pallas_call(
        tail_kernel,
        out_shape=jax.ShapeDtypeStruct((ctx_count, 24, LANES), BF16),
        in_specs=[VM] * 4,
        out_specs=VM,
        compiler_params=PARAMS,
        name="tails",
    )(q_one, k_one, v_one, short_taps)
    spread = lax.all_to_all(tails, "ctx", split_axis=0, concat_axis=0, tiled=True)
    fetched = lax.all_to_all(jnp.take(spread, source, axis=0), "ctx", split_axis=0, concat_axis=0, tiled=True)
    flag = block_order[me].reshape(1)
    mixed, energy = pl.pallas_call(
        mix_kernel,
        out_shape=(jax.ShapeDtypeStruct((width, rows), F32), jax.ShapeDtypeStruct((1, rows), F32)),
        in_specs=[SM] + [VM] * 7,
        out_specs=(VM, VM),
        scratch_shapes=[
            pltpu.VMEM((8 * LANES, 2 * LANES), BF16),
            pltpu.VMEM((8 + rows, LANES), F32),
            pltpu.VMEM((LANES + rows, LANES), BF16),
        ],
        compiler_params=PARAMS,
        name="mix",
    )(flag, q_one, k_one, v_one, k_two, short_taps, medium_taps, fetched)
    energy = lax.psum(energy, "tp")
    v_two = (mixed * lax.rsqrt(energy / full_width + EPSILON)).astype(BF16)
    received = lax.all_to_all(v_two.reshape(ctx_count, lane_width, rows), "ctx", split_axis=0, concat_axis=0, tiled=True)
    gain = lax.dynamic_slice_in_dim(skip_gain, me * lane_width, lane_width).reshape(lane_width, 1)
    size = ctx_count * lane_width
    mixed_seq = pl.pallas_call(
        long_kernel,
        out_shape=jax.ShapeDtypeStruct((ctx_count, lane_width, rows), BF16),
        in_specs=[SM] * 2 + [VM] * 3,
        out_specs=VM,
        scratch_shapes=[
            pltpu.VMEM((size + size // 4, rows), BF16),
            pltpu.VMEM((LANES, LANES + ctx_count * rows), BF16),
            pltpu.VMEM((size // 4, rows), F32),
        ],
        compiler_params=PARAMS,
        name="long",
    )(holder, block_order, received, long_rows, gain)
    returned = lax.all_to_all(jnp.take(mixed_seq, block_order, axis=0), "ctx", split_axis=0, concat_axis=0, tiled=True)
    return pl.pallas_call(
        gate_kernel,
        out_shape=jax.ShapeDtypeStruct((rows, width), BF16),
        in_specs=[VM] * 2,
        out_specs=VM,
        compiler_params=PARAMS,
        name="gate",
    )(returned, q_two)


def solution(mesh):
    in_specs = (
        P("ctx", "tp"),
        P("ctx", "tp"),
        P("ctx", "tp"),
        P("ctx", "tp"),
        P("ctx", "tp"),
        P(None, None, "tp"),
        P(None, "tp"),
        P("tp", "ctx"),
        P("tp"),
        P(),
        P(),
    )
    return jax.shard_map(per_device, mesh=mesh, in_specs=in_specs, out_specs=P("ctx", "tp"), check_vma=False)
```

```python
import functools

import jax
import jax.numpy as jnp
from jax import lax
from jax.experimental import pallas as pl
from jax.experimental.pallas import tpu as pltpu
from jax.sharding import PartitionSpec as P

EPSILON = 1e-06
LANES = 128
GROUP = 16
LEAD = 6
TILES = 8
STEP = 4
F32 = jnp.float32
BF16 = jnp.bfloat16
MESH = pl.DeviceIdType.MESH


def iota(shape, dim):
    return lax.broadcasted_iota(jnp.int32, shape, dim)


def skewed(row):
    return pltpu.roll(jnp.broadcast_to(row, (LANES, LANES)), 0, 1, stride=1, stride_axis=0)


def tile_lanes(tile):
    return pl.ds(pl.multiple_of(tile * LANES, LANES), LANES)


def hyena_kernel(
    n_ctx, n_tp, full_width,
    order_ref, prev_ref, q_hbm, k_hbm, v_hbm, q_two_hbm, k_two_hbm, short_ref, medium_ref, long_ref, gain_ref,
    out_ref,
    q_in, k_in, v_in, q_two, k_two, taps, turned, signal, edge, q_feat, k_head, v_head, z_pad, medium_toe, long_toe, long_f32,
    send_one, recv_one, send_two, recv_two, send_u, recv_u, part, part_recv, scale, scale_recv, spread, total, in_order, send_y, recv_y,
    in_sem, one_send, one_recv, two_send, two_recv, u_send, u_recv, part_send, part_sem, scale_send, scale_sem, y_send, y_recv,
):
    rows, width = q_in.shape
    me = lax.axis_index("ctx")
    my_tp = lax.axis_index("tp")
    my_group = me // TILES

    def peer(i):
        return lax.rem(me + i, n_ctx)

    barrier = pltpu.get_barrier_semaphore()

    def greet(i, carry):
        pl.semaphore_signal(barrier, inc=1, device_id={"ctx": peer(i)}, device_id_type=MESH)
        return carry

    lax.fori_loop(1, n_ctx, greet, 0)
    for i in range(1, n_tp):
        pl.semaphore_signal(barrier, inc=1, device_id={"tp": lax.rem(my_tp + i, n_tp)}, device_id_type=MESH)

    loads = [
        pltpu.make_async_copy(src, dst, in_sem.at[i])
        for i, (src, dst) in enumerate(((q_hbm, q_in), (k_hbm, k_in), (v_hbm, v_in), (q_two_hbm, q_two), (k_two_hbm, k_two)))
    ]
    for load in loads:
        load.start()

    groups = short_ref.shape[2]
    pick = (iota((groups, width), 0) == iota((groups, width), 1) // GROUP).astype(F32)
    for which in range(3):
        taps[which, 0 : LEAD + 1, :] = jnp.dot(short_ref[which].astype(F32), pick, preferred_element_type=F32)
    flip = (iota((LANES, LANES), 0) == (LANES - iota((LANES, LANES), 1)) % LANES).astype(F32)
    turned[...] = jnp.dot(medium_ref[...].astype(F32), flip, preferred_element_type=F32)
    long_f32[...] = long_ref[...].astype(F32)
    edge[...] = jnp.zeros(edge.shape, F32)
    signal[0:8, :] = jnp.zeros((8, LANES), F32)
    spread[0 : STEP * GROUP, :] = jnp.zeros((STEP * GROUP, spread.shape[1]), BF16)
    for load in loads[:3]:
        load.wait()

    def local_step(tile, carry):
        lanes = tile_lanes(tile)
        features = []
        for which, ref in enumerate((q_in, k_in, v_in)):
            signal[8 : 8 + rows, :] = ref[:, lanes].astype(F32)
            tap = taps[which, :, lanes]
            feature = jnp.zeros((rows, LANES), F32)
            for j in range(LEAD + 1):
                feature += signal[8 - j : 8 - j + rows, :] * tap[j : j + 1]
            features.append(feature)
        q_feat[tile] = features[0]
        k_head[tile] = features[1][:GROUP]
        v_head[tile] = features[2][:GROUP]
        z_pad[tile, LANES : LANES + rows, :] = (features[1] * features[2]).astype(BF16)
        ends = [ref[rows - 8 :, lanes].astype(F32)[8 - LEAD :] for ref in (q_in, k_in, v_in)]
        ends = jnp.concatenate(ends + [jnp.zeros((6, LANES), F32)], axis=0)
        for a in range(TILES):
            send_one[a * TILES + tile, 0:16, :] = z_pad[tile, rows + 16 * a : rows + 16 * a + 16, :]
            long_row = long_f32[pl.ds(a * TILES + tile, 1), :]
            piece = [ends[3 * a : 3 * a + 3], long_row[:, :LANES], long_row[:, LANES:], jnp.zeros((3, LANES), F32)]
            send_one[a * TILES + tile, 16:24, :] = jnp.concatenate(piece, axis=0).astype(BF16)
        return carry

    lax.fori_loop(0, TILES, local_step, 0)
    pl.semaphore_wait(barrier, n_ctx - 1 + n_tp - 1)

    def send_all(source, target, send_sem, recv_sem):
        def send(i, carry):
            p = peer(i)
            pltpu.make_async_remote_copy(
                source.at[p], target.at[me], send_sem, recv_sem, device_id={"ctx": p}, device_id_type=MESH
            ).start()
            return carry

        lax.fori_loop(1, n_ctx, send, 0)

    def wait_for(ref, count, sem):
        view = ref.at[pl.ds(0, count)]
        pltpu.make_async_copy(view, view, sem).wait()

    send_all(send_one, recv_one, one_send, one_recv)
    recv_one[me] = send_one[me]

    row_at, col_at = iota((LANES, LANES), 0), iota((LANES, LANES), 1)

    def medium_step(tile, carry):
        for g in range(TILES):
            skew = skewed(turned[pl.ds(tile * TILES + g, 1), :])
            at = pl.ds(g * LANES, LANES)
            medium_toe[tile, at, 0:LANES] = jnp.where(col_at > row_at, skew, 0.0).astype(BF16)
            medium_toe[tile, at, LANES : 2 * LANES] = jnp.where(col_at <= row_at, skew, 0.0).astype(BF16)
        return carry

    lax.fori_loop(0, TILES, medium_step, 0)

    wait_for(recv_one, n_ctx - 1, one_recv)

    def route(d, carry):
        send_two[d] = recv_one[prev_ref[order_ref[d]]]
        return carry

    lax.fori_loop(0, n_ctx, route, 0)
    recv_two[me] = recv_one[prev_ref[order_ref[me]]]
    send_all(send_two, recv_two, two_send, two_recv)

    long_toe[:, 0:LANES] = jnp.zeros((LANES, LANES), BF16)

    def long_step(k, last):
        row = recv_one[k, 16:24, :].astype(F32)
        first, second = skewed(row[3:4]), skewed(row[4:5])
        at = pl.multiple_of(LANES + k * rows, LANES)
        long_toe[:, pl.ds(at, LANES)] = jnp.where(col_at >= row_at, first, last).astype(BF16)
        long_toe[:, pl.ds(at + LANES, LANES)] = jnp.where(col_at >= row_at, second, first).astype(BF16)
        return second

    lax.fori_loop(0, n_ctx, long_step, jnp.zeros((LANES, LANES), F32))
    loads[3].wait()
    loads[4].wait()
    wait_for(recv_two, n_ctx - 1, two_recv)

    before = jnp.minimum(order_ref[me], 1).astype(F32)
    owner = iota((LANES, 2 * LANES), 1) % LANES // GROUP

    def mix_step(i, energy):
        tile = lax.rem(my_group + i, TILES)
        lanes = tile_lanes(tile)
        ends = jnp.concatenate([recv_two[a * TILES + tile, 16:24, :].astype(F32)[:3] for a in range(6)], axis=0) * before
        heads = []
        for which, head in enumerate((q_feat[tile, 0:GROUP, :], k_head[tile], v_head[tile])):
            edge[0:8, :] = jnp.concatenate([jnp.zeros((8 - LEAD, LANES), F32), ends[which * LEAD : (which + 1) * LEAD]], axis=0)
            tap = taps[which, :, lanes]
            for j in range(LEAD + 1):
                head += edge[8 - j : 8 - j + GROUP, :] * tap[j : j + 1]
            heads.append(head)
        q_feat[tile, 0:GROUP, :] = heads[0]
        z_pad[tile, LANES : LANES + GROUP, :] = (heads[1] * heads[2]).astype(BF16)
        for a in range(TILES):
            z_pad[tile, 16 * a : 16 * a + 16, :] = (recv_two[a * TILES + tile, 0:16, :].astype(F32) * before).astype(BF16)
        stacked = jnp.concatenate([z_pad[tile, 0:rows, :], z_pad[tile, LANES : LANES + rows, :]], axis=1)
        product = jnp.dot(medium_toe[tile], stacked, preferred_element_type=F32)
        medium = jnp.zeros((LANES, 2 * LANES), F32)
        for g in range(TILES):
            medium = jnp.where(owner == g, product[g * LANES : (g + 1) * LANES], medium)
        medium = jnp.concatenate([medium[:, :LANES], medium[:, LANES:]], axis=0)
        mixed = q_feat[tile] * medium
        sent = jnp.transpose(mixed * k_two[:, lanes].astype(F32)).astype(BF16)
        send_u[pl.ds(tile * TILES, TILES)] = sent.reshape(TILES, GROUP, rows)
        energy = energy + mixed * mixed

        def send(j, carry):
            p = tile * TILES + lax.rem(me + j, TILES)

            @pl.when(p != me)
            def _():
                pltpu.make_async_remote_copy(
                    send_u.at[p], recv_u.at[me], u_send, u_recv, device_id={"ctx": p}, device_id_type=MESH
                ).start()

            return carry

        lax.fori_loop(0, TILES, send, 0)
        return energy

    energy = lax.fori_loop(0, width // LANES, mix_step, jnp.zeros((rows, LANES), F32))
    recv_u[me] = send_u[me]

    part[...] = jnp.sum(jnp.transpose(energy), axis=0, keepdims=True)
    for i in range(1, n_tp):
        pltpu.make_async_remote_copy(
            part, part_recv.at[i - 1], part_send, part_sem, device_id={"tp": lax.rem(my_tp + i, n_tp)}, device_id_type=MESH
        ).start()
    wait_for(part_recv, n_tp - 1, part_sem)
    whole = part[...]
    for i in range(1, n_tp):
        whole = whole + part_recv[i - 1]
    scale[...] = lax.rsqrt(whole / full_width + EPSILON)
    scale_recv[me] = scale[...]

    def send_scale(i, carry):
        p = peer(i)
        pltpu.make_async_remote_copy(
            scale, scale_recv.at[me], scale_send, scale_sem, device_id={"ctx": p}, device_id_type=MESH
        ).start()
        return carry

    lax.fori_loop(1, n_ctx, send_scale, 0)
    gain_row = jnp.broadcast_to(gain_ref[pl.ds(my_group, 1), :], (GROUP, LANES))
    gain_at = iota((GROUP, LANES), 1) == lax.rem(me, TILES) * GROUP + iota((GROUP, LANES), 0)
    gain = jnp.sum(jnp.where(gain_at, gain_row, 0.0), axis=1, keepdims=True)
    wait_for(recv_u, n_ctx - 1, u_recv)
    wait_for(scale_recv, n_ctx - 1, scale_sem)

    def place(b, carry):
        holder = prev_ref[lax.rem(b + 1, n_ctx)]
        value = (recv_u[holder].astype(F32) * scale_recv[holder]).astype(BF16)
        total[pl.ds(pl.multiple_of(b * GROUP, GROUP), GROUP), :] = value.astype(F32) * gain
        for s in range(STEP):
            spread[pl.ds(pl.multiple_of((b + s) * GROUP, GROUP), GROUP), s * rows : (s + 1) * rows] = value
        return carry

    lax.fori_loop(0, n_ctx, place, 0)
    for n in range(n_ctx // STEP):
        count = (n_ctx - n * STEP) * GROUP
        band = []
        for s in range(STEP):
            at = LANES + (n * STEP + s) * rows
            band += [long_toe[:, at : at + rows], long_toe[:, at - LANES : at - LANES + rows]]
        total[n * STEP * GROUP :, :] += jnp.dot(spread[0:count, :], jnp.concatenate(band, axis=0), preferred_element_type=F32)

    in_order[...] = total[...].astype(BF16).reshape(in_order.shape)

    def give(d, carry):
        send_y[d] = in_order[order_ref[d]]
        return carry

    lax.fori_loop(0, n_ctx, give, 0)

    def send_back(i, carry):
        p = peer(i)
        pltpu.make_async_remote_copy(
            send_y.at[p], recv_y.at[me], y_send, y_recv.at[my_group], device_id={"ctx": p}, device_id_type=MESH
        ).start()
        return carry

    lax.fori_loop(1, n_ctx, send_back, 0)
    recv_y[me] = send_y[me]

    def gate(tile):
        lanes = tile_lanes(tile)
        piece = recv_y[pl.ds(tile * TILES, TILES)].astype(F32).reshape(LANES, rows)
        out_ref[:, lanes] = (jnp.transpose(piece) * q_two[:, lanes].astype(F32)).astype(BF16)

    def gate_step(i, carry):
        tile = lax.rem(my_group + TILES - i, TILES)
        wait_for(recv_y, TILES, y_recv.at[tile])
        gate(tile)
        return carry

    lax.fori_loop(1, TILES, gate_step, 0)
    wait_for(recv_y, TILES - 1, y_recv.at[my_group])
    gate(my_group)
    wait_for(send_one, n_ctx - 1, one_send)
    wait_for(send_two, n_ctx - 1, two_send)
    wait_for(send_u, n_ctx - 1, u_send)
    wait_for(part_recv, n_tp - 1, part_send)
    wait_for(scale_recv, n_ctx - 1, scale_send)
    wait_for(send_y, n_ctx - 1, y_send)


def per_device(q_one, k_one, v_one, q_two, k_two, short_taps, medium_taps, long_taps, skip_gain, block_order, prev_owner):
    rows, width = q_one.shape
    n_ctx, n_tp = lax.axis_size("ctx"), lax.axis_size("tp")
    span = n_ctx * rows
    VM, SM, ANY = (pl.BlockSpec(memory_space=s) for s in (pltpu.VMEM, pltpu.SMEM, pl.ANY))
    vmem = pltpu.VMEM
    dma = pltpu.SemaphoreType.DMA
    return pl.pallas_call(
        functools.partial(hyena_kernel, n_ctx, n_tp, width * n_tp),
        out_shape=jax.ShapeDtypeStruct((rows, width), BF16),
        in_specs=[SM] * 2 + [ANY] * 5 + [VM] * 4,
        out_specs=VM,
        scratch_shapes=[vmem((rows, width), BF16)] * 5
        + [
            vmem((3, 8, width), F32),
            vmem((width // GROUP, LANES), F32),
            vmem((8 + rows, LANES), F32),
            vmem((8 + GROUP, LANES), F32),
            vmem((TILES, rows, LANES), F32),
            vmem((TILES, GROUP, LANES), F32),
            vmem((TILES, GROUP, LANES), F32),
            vmem((TILES, LANES + rows, LANES), BF16),
            vmem((TILES, TILES * LANES, 2 * LANES), BF16),
            vmem((LANES, LANES + span), BF16),
            vmem((n_ctx, rows), F32),
        ]
        + [vmem((n_ctx, 24, LANES), BF16)] * 4
        + [vmem((n_ctx, GROUP, rows), BF16)] * 2
        + [
            vmem((1, rows), F32),
            vmem((n_tp - 1, 1, rows), F32),
            vmem((1, rows), F32),
            vmem((n_ctx, 1, rows), F32),
            vmem(((n_ctx + STEP) * GROUP, STEP * rows), BF16),
            vmem((n_ctx * GROUP, rows), F32),
        ]
        + [vmem((n_ctx, GROUP, rows), BF16)] * 3
        + [dma((5,))]
        + [dma] * 11
        + [dma((TILES,))],
        compiler_params=pltpu.CompilerParams(collective_id=0, has_side_effects=True, vmem_limit_bytes=60 * 1024 * 1024),
        name="hyena",
    )(
        block_order, prev_owner, q_one, k_one, v_one, q_two, k_two,
        short_taps, jnp.transpose(medium_taps), long_taps, skip_gain.reshape(width // LANES, LANES),
    )


def solution(mesh):
    in_specs = (
        P("ctx", "tp"),
        P("ctx", "tp"),
        P("ctx", "tp"),
        P("ctx", "tp"),
        P("ctx", "tp"),
        P(None, None, "tp"),
        P(None, "tp"),
        P("tp", "ctx"),
        P("tp"),
        P(),
        P(),
    )
    return jax.shard_map(per_device, mesh=mesh, in_specs=in_specs, out_specs=P("ctx", "tp"), check_vma=False)
```
